512 devices in a mesh: dp: 64 (over y, z_lo, core), tensor: 8 (over z_hi, x).
Axes of the slice: x: 4, y: 8, z: 8 (z_hi: 2, z_lo: 4; z = z_hi * 4 + z_lo), core: 2. Of those that a mesh axis runs over, the one named last changes fastest.
Arguments:
- layer_input: bfloat16 [2, 4096, 8192], P(None, ('dp', 'tensor')), may hold values from -6 to 6
- key_gradient_rows: bfloat16 [2, 4096, 1024], P(None, 'dp', 'tensor'), may hold values from -6 to 6
- key_block_matrix: bfloat16 [8, 6144, 128], P('tensor', 'dp'), may hold values from -0.09375 to 0.09375
- kept_rows: int32 [8, 48], replicated, may hold values from -1 to 63, as said below
Outputs:
- weight_grad: float32 [8, 6144, 128], P('tensor', 'dp')
- input_grad: bfloat16 [2, 4096, 8192], P(None, ('dp', 'tensor'))
The draws below stay inside these ranges and needn't reach their ends.
Inputs may be any that keep to these rules, and one draw needn't show every extreme that they name: `kept_rows`: row h lists in ascending order the distinct blocks (of the 64 blocks of 128 input rows) that survive pruning for head h, then -1 in its unused slots. At most 48 blocks survive for one head and exactly 48 for some head; 256 blocks survive in all, at least one for every head.
All inputs are finite; a program needn't handle non-finite values.
Results may differ from the reference program's by a relative error of at most 0.005.
Values may be sent and summed in bfloat16 or wider, within the bound.
A program may use at most 64 MiB of HBM per device.

```python
import math
import jax
import jax.numpy as jnp

MODEL_WIDTH = 8192
HEAD_WIDTH = 128
PRUNE_BLOCK_ROWS = 128
HEAD_BLOCK_LIMIT = 48
MICRO_BATCHES = 2
KEY_VALUE_HEADS = 8
MICRO_TOKENS = 4096


def draw_kept_rows(key, part):
    block_count = MODEL_WIDTH // PRUNE_BLOCK_ROWS
    grand_sum = KEY_VALUE_HEADS * block_count // 2
    remaining_heads = KEY_VALUE_HEADS - 1
    rest = grand_sum - HEAD_BLOCK_LIMIT
    base = rest // remaining_heads
    extra = rest % remaining_heads
    key_occupied, key_shift, key_reordering = jax.random.split(key, 3)
    spread = max(0, min(base - 1, HEAD_BLOCK_LIMIT - base - 1))
    pairing = jnp.arange(remaining_heads)
    counts_other = base + (pairing < extra).astype(jnp.int32)
    shifts = jax.random.randint(key_shift, (remaining_heads,), -spread, spread + 1)
    paired = pairing < 2 * (remaining_heads // 2)
    signs = jnp.where(pairing % 2 == 0, 1, -1)
    counts_other = counts_other + jnp.where(paired, signs * shifts[pairing - pairing % 2], 0)
    occupied_slots = jax.random.randint(key_occupied, (), 0, KEY_VALUE_HEADS)
    every_head_list = jnp.arange(KEY_VALUE_HEADS)
    source = jnp.clip(every_head_list - (every_head_list > occupied_slots).astype(jnp.int32), 0, remaining_heads - 1)
    counts = jnp.where(every_head_list == occupied_slots, HEAD_BLOCK_LIMIT, counts_other[source]).astype(jnp.int32)
    key_rows_list = jax.random.split(key_reordering, KEY_VALUE_HEADS)

    def one_order(single):
        return jax.random.permutation(single, block_count)
    orders = jax.vmap(one_order)(key_rows_list)
    chosen = (orders[:, :, None] == jnp.arange(block_count)[None, None, :]) & (jnp.arange(block_count)[None, :, None] < counts[:, None, None])
    member = jnp.any(chosen, axis=1)
    slot_of = jnp.cumsum(member.astype(jnp.int32), axis=1) - 1
    match = member[:, :, None] & (slot_of[:, :, None] == jnp.arange(HEAD_BLOCK_LIMIT)[None, None, :])
    rows_found = jnp.sum(jnp.where(match, jnp.arange(block_count)[None, :, None], 0), axis=1)
    filled = jnp.arange(HEAD_BLOCK_LIMIT)[None, :] < counts[:, None]
    return jnp.where(filled, rows_found, -1).astype(jnp.int32)


def levels(stream_key, extent, pieces, smallest, top_value):
    factor_of = 1.0
    for position, shards_of in pieces:
        draws = jax.random.uniform(jax.random.fold_in(jax.random.fold_in(stream_key, 6), position), (shards_of,), jnp.float32, smallest / len(pieces), top_value / len(pieces))
        factor_of = factor_of * jnp.repeat(jnp.exp(draws), extent[position] // shards_of).reshape((-1,) + (1,) * (len(extent) - 1 - position))
    return factor_of


def noise(stream_key, shape, width, most, cuts=(), held_as=jnp.bfloat16):
    array = width * jax.random.normal(stream_key, shape, jnp.float32)
    if cuts:
        array = array * levels(stream_key, shape, cuts, -0.22, 0.18)
    return jnp.clip(array, -most, most).astype(held_as)


def setup_inputs(seed: int = 0) -> dict:
    splits = jax.random.split(jax.random.key(seed), 5)
    layer_input = noise(splits[0], (MICRO_BATCHES, MICRO_TOKENS, MODEL_WIDTH), 1.0, 6.0, ((1, 512),))
    key_gradient_rows = noise(splits[1], (MICRO_BATCHES, MICRO_TOKENS, KEY_VALUE_HEADS * HEAD_WIDTH), 1.0, 6.0, ((1, 64), (2, 8)))
    key_block_matrix = noise(splits[2], (KEY_VALUE_HEADS, HEAD_BLOCK_LIMIT * PRUNE_BLOCK_ROWS, HEAD_WIDTH), (MODEL_WIDTH // 2) ** -0.5, 0.09375, ((0, 8), (1, 64)))
    kept_rows = draw_kept_rows(jax.random.fold_in(splits[4], 71), 0)
    return {"layer_input": layer_input, "key_gradient_rows": key_gradient_rows, "key_block_matrix": key_block_matrix, "kept_rows": kept_rows}


def reference(layer_input, key_gradient_rows, key_block_matrix, kept_rows):
    head_count = kept_rows.shape[0]
    block_count = MODEL_WIDTH // PRUNE_BLOCK_ROWS
    alive = kept_rows >= 0
    clipped = jnp.maximum(kept_rows, 0).astype(jnp.int32)
    blocks_w = key_block_matrix.reshape(head_count, HEAD_BLOCK_LIMIT, PRUNE_BLOCK_ROWS, HEAD_WIDTH) * alive[:, :, None, None].astype(jnp.bfloat16)
    full_grad = jnp.zeros((MODEL_WIDTH, head_count * HEAD_WIDTH), jnp.float32)
    for micro in range(MICRO_BATCHES):
        full_grad = full_grad + jnp.dot(layer_input[micro].T, key_gradient_rows[micro], preferred_element_type=jnp.float32)
    full_grad = full_grad.reshape(block_count, PRUNE_BLOCK_ROWS, head_count, HEAD_WIDTH)
    scale = 1.0 / math.sqrt(MICRO_BATCHES * MICRO_TOKENS)
    grad_list = []
    for which in range(head_count):
        picked = jnp.take(full_grad[:, :, which, :], clipped[which], axis=0)
        grad_list.append(picked * alive[which][:, None, None].astype(jnp.float32))
    weight_grad = jnp.stack(grad_list).reshape(head_count, HEAD_BLOCK_LIMIT * PRUNE_BLOCK_ROWS, HEAD_WIDTH) * scale
    results = []
    for micro in range(MICRO_BATCHES):
        summed = jnp.zeros((MICRO_TOKENS, block_count, PRUNE_BLOCK_ROWS), jnp.float32)
        for which in range(head_count):
            grads_here = key_gradient_rows[micro][:, which * HEAD_WIDTH:(which + 1) * HEAD_WIDTH]
            partial_value = jnp.dot(grads_here, blocks_w[which].reshape(HEAD_BLOCK_LIMIT * PRUNE_BLOCK_ROWS, HEAD_WIDTH).T, preferred_element_type=jnp.float32).astype(jnp.bfloat16)
            summed = summed.at[:, clipped[which], :].add(partial_value.reshape(MICRO_TOKENS, HEAD_BLOCK_LIMIT, PRUNE_BLOCK_ROWS).astype(jnp.float32))
        results.append(summed.reshape(MICRO_TOKENS, MODEL_WIDTH).astype(jnp.bfloat16))
    return (weight_grad, jnp.stack(results))
```

```python
import math

import jax
import jax.numpy as jnp
from jax import lax
from jax.experimental import pallas as pl
from jax.experimental.pallas import tpu as pltpu
from jax.sharding import PartitionSpec as P

MODEL_WIDTH = 8192
HEAD_WIDTH = 128
BLOCK = 128
SLOTS = 48
BLOCKS = MODEL_WIDTH // BLOCK
MICRO = 2
N = 8
XN = 4
SHARD = SLOTS * BLOCK // 64
HALF = SHARD // 2
UNIT = 16
PER = BLOCK // UNIT
SHARD_UNITS = SHARD // UNIT
HEAD_UNITS = SLOTS * PER
HEAD_STRIDE = HEAD_UNITS + PER
DENSE_STRIDE = BLOCKS * PER + PER
OWN = 16
GROUP = MODEL_WIDTH // 4
MESH = pl.DeviceIdType.MESH
OFFSETS = (0, 1, -1, 2, -2, 3, -3, 4)
AT = {offset: index for index, offset in enumerate(OFFSETS)}
DIRECTIONS = ((0, 1), (1, -1))
X_ORDER = ((0, 1, 2, 3, 0, 1), (2, 3, 0, 1, 2, 3))
f32, bf16 = jnp.float32, jnp.bfloat16


def wrap(value, size):
    return lax.rem(value + size, size)


def kernel(
    kept, slot_of, x_in, k_in, w_in, w_out, x_out,
    w_all, x_all, k_raw, k_hop, k_cat, dense, part, got, total, got2, send2, og, xr, xa,
    local_sem, a_send, a_recv, b_send, b_recv, pw_send, pw_recv, px_send, px_recv, pk_send, pk_recv,
    x_send, x_recv, kc_send, kc_recv, r_send, r_recv, s_send, s_recv, o_send, o_recv,
):
    dp, tp = lax.axis_index("dp"), lax.axis_index("tensor")
    y, zl, core = dp // 8, lax.rem(dp // 2, 4), lax.rem(dp, 2)
    zh, xx = tp // 4, lax.rem(tp, 4)
    z = zh * 4 + zl
    a = y + core * (z - y)
    b = z + core * (y - z)

    def device(y_, z_, core_, x_):
        return (y_ * 8 + lax.rem(z_, 4) * 2 + core_, (z_ // 4) * 4 + x_)

    def device_ab(a_, b_):
        return device(a_ + core * (b_ - a_), b_ + core * (a_ - b_), core, xx)

    a_at = {o: wrap(a + o, N) for o in OFFSETS}
    b_at = {o: wrap(b + o, N) for o in OFFSETS}

    def y_rows(y_):
        return y_ * (768 // UNIT)

    def z_rows(z_):
        return (z_ // 4) * HEAD_STRIDE + PER + lax.rem(z_, 4) * (192 // UNIT)

    a_rows = {o: y_rows(v) + core * (z_rows(v) - y_rows(v)) + core * SHARD_UNITS for o, v in a_at.items()}
    b_rows = {o: z_rows(v) + core * (y_rows(v) - z_rows(v)) for o, v in b_at.items()}
    to_a = {d: device_ab(a_at[d], b) for d in (1, -1)}
    to_b = {d: device_ab(a, b_at[d]) for d in (1, -1)}
    to_z = {d: device(y, wrap(z + d, N), core, xx) for d in (1, -1)}
    to_x = {d: device(y, z, core, wrap(xx + d, XN)) for d in (1, -1)}
    to_y = {d: device(wrap(y + d, N), z, core, xx) for d in (1, -1)}
    partner = device(y, z, 1 - core, xx)

    barrier = pltpu.get_barrier_semaphore()
    for there in (to_y[1], to_y[-1], to_z[1], to_z[-1], to_x[1], to_x[-1], partner):
        pl.semaphore_signal(barrier, inc=1, device_id=there, device_id_type=MESH)

    def remote(src, dst, send, recv, there):
        return pltpu.make_async_remote_copy(
            src_ref=src, dst_ref=dst, send_sem=send, recv_sem=recv, device_id=there, device_id_type=MESH
        )

    def piece(oa, ob, half=None):
        row = a_rows[oa] + b_rows[ob]
        if half is None:
            return w_all.at[pl.ds(row, SHARD_UNITS)]
        return w_all.at[pl.ds(row + half * (SHARD_UNITS // 2), SHARD_UNITS // 2)]

    def ring_offset(d, hop):
        return 4 if hop == 4 else -d * hop

    def a_copy(i, d, hop):
        offset = -d * (hop - 1)
        half = i if hop == 4 else None
        src = w_in if hop == 1 else piece(offset, 0, half)
        return remote(src, piece(offset, 0, half), a_send.at[i, hop - 1], a_recv.at[i, hop - 1], to_a[d])

    def b_copy(oa, i, d, hop):
        offset = -d * (hop - 1)
        half = i if hop == 4 else None
        src = w_in if hop == 1 and oa == 0 else piece(oa, offset, half)
        j = AT[oa]
        return remote(
            src, piece(oa, offset, half), b_send.at[j, i, hop - 1], b_recv.at[j, i, hop - 1], to_b[d]
        )

    def share(oa, ob, half=None, src=None):
        ref = piece(oa, ob, half)
        remote(ref if src is None else src, ref, pw_send, pw_recv, partner).start()

    def x_rows(core_, x_):
        return pl.ds(pl.multiple_of(core_ * 64 + x_ * OWN, OWN), OWN)

    def x_columns(group):
        return pl.ds(group * GROUP, GROUP)

    def x_copy(i, d, n):
        columns = x_columns(X_ORDER[i][n])
        if n < 4:
            src, origin = x_in.at[:, columns], xx
        else:
            origin = wrap(xx - d, XN)
            src = x_all.at[x_rows(core, origin), columns]
        return remote(
            src, x_all.at[x_rows(core, origin), columns], x_send.at[i, n], x_recv.at[i, n], to_x[d]
        )

    def share_x(i, d, n):
        origin = wrap(xx - d, XN) if n < 4 else wrap(xx - 2 * d, XN)
        ref = x_all.at[x_rows(core, origin), x_columns(X_ORDER[i][n])]
        remote(ref, ref, px_send, px_recv, partner).start()

    def k_copy(i, d, hop):
        if hop == 1:
            src = k_in.at[i, pl.ds(pl.multiple_of((1 - zh) * 32, 32), 32)]
        else:
            src = k_hop.at[i, hop - 2]
        if hop == 4:
            dst = k_raw.at[core, 1 - wrap(z + d, N) // 4, i]
        else:
            dst = k_hop.at[i, hop - 1]
        return remote(src, dst, kc_send.at[i, hop - 1], kc_recv.at[i, hop - 1], to_z[d])

    def k_share(own):
        if own:
            src = k_in.at[:, pl.ds(pl.multiple_of(zh * 32, 32), 32)]
            return remote(src, k_raw.at[core, zh], pk_send.at[0], pk_recv.at[0], partner)
        ref = k_raw.at[core, 1 - zh]
        return remote(ref, ref, pk_send.at[1], pk_recv.at[1], partner)

    local = [
        pltpu.make_async_copy(w_in, piece(0, 0), local_sem.at[0]),
        pltpu.make_async_copy(x_in, x_all.at[x_rows(core, xx)], local_sem.at[1]),
        pltpu.make_async_copy(
            k_in.at[:, pl.ds(pl.multiple_of(zh * 32, 32), 32)], k_raw.at[core, zh], local_sem.at[2]
        ),
    ]
    for copy in local:
        copy.start()
    for head in range(2):
        w_all[pl.ds(head * HEAD_STRIDE, PER)] = jnp.zeros((PER, UNIT, HEAD_WIDTH), bf16)
        dense[pl.ds(head * DENSE_STRIDE, PER)] = jnp.zeros((PER, UNIT, HEAD_WIDTH), bf16)

    pl.semaphore_wait(barrier, 7)

    for i, d in DIRECTIONS:
        a_copy(i, d, 1).start()
        b_copy(0, i, d, 1).start()
        k_copy(i, d, 1).start()
    for n in range(4):
        for i, d in DIRECTIONS:
            x_copy(i, d, n).start()
    share(0, 0, src=w_in)
    k_share(True).start()
    remote(x_in, x_all.at[x_rows(core, xx)], px_send, px_recv, partner).start()

    def a_arrival(step):
        for i, d in DIRECTIONS:
            a_copy(i, d, step).wait_recv()
            if step < 4:
                a_copy(i, d, step + 1).start()
                for i2, d2 in DIRECTIONS:
                    b_copy(-d * step, i2, d2, 1).start()
                share(-d * step, 0)
        if step == 4:
            for i2, d2 in DIRECTIONS:
                b_copy(4, i2, d2, 1).start()
            share(4, 0)

    def b_arrival(oa, hop):
        for i, d in DIRECTIONS:
            b_copy(oa, i, d, hop).wait_recv()
            if hop < 4:
                b_copy(oa, i, d, hop + 1).start()
                share(oa, -d * hop)
            else:
                share(oa, 4, i)

    for step in range(1, 9):
        if step <= 4:
            a_arrival(step)
        for oa in OFFSETS:
            hop = step - abs(oa)
            if 1 <= hop <= 4:
                b_arrival(oa, hop)
        if step <= 4:
            for i, d in DIRECTIONS:
                k_copy(i, d, step).wait_recv()
                if step < 4:
                    k_copy(i, d, step + 1).start()
            if step == 4:
                k_share(False).start()
        if step in (2, 3, 5, 6):
            n = {2: 0, 3: 1, 5: 2, 6: 3}[step]
            for i, d in DIRECTIONS:
                x_copy(i, d, n).wait_recv()
                if n < 2:
                    x_copy(i, d, n + 4).start()
                share_x(i, d, n)
    for n in (4, 5):
        for i, d in DIRECTIONS:
            x_copy(i, d, n).wait_recv()
            share_x(i, d, n)

    for copy in local:
        copy.wait()
    k_share(True).wait()
    k_share(False).wait()
    for core_ in range(2):
        for head in range(2):
            raw = k_raw[core_, head].astype(f32)
            rows = [raw[m, x_ * 8:x_ * 8 + 8] for x_ in range(XN) for m in range(MICRO)]
            k_cat[core_ * 64:core_ * 64 + 64, head * 128:head * 128 + 128] = jnp.concatenate(
                rows, axis=0
            ).astype(bf16)
    x_shared = x_all.at[pl.ds(0, 64)]
    remote(x_shared, x_shared, px_send, px_recv, partner).wait()

    width = 512

    def dense_step(step, carry):
        columns = pl.ds(pl.multiple_of(step * width, width), width)
        product = lax.dot_general(
            x_all[:, columns], k_cat[...], (((0,), (0,)), ((), ())), preferred_element_type=f32
        ).astype(bf16)
        for head in range(2):
            rows = pl.ds(head * DENSE_STRIDE + PER + step * (width // UNIT), width // UNIT)
            dense[rows] = product[:, head * 128:head * 128 + 128].reshape(width // UNIT, UNIT, HEAD_WIDTH)
        return carry

    lax.fori_loop(0, MODEL_WIDTH // width, dense_step, 0)

    def pick(ob):
        for oa in OFFSETS:
            y_ = a_at[oa] + core * (b_at[ob] - a_at[oa])
            z_ = b_at[ob] + core * (a_at[oa] - b_at[ob])
            head = z_ // 4
            first = y_ * 48 + lax.rem(z_, 4) * 12 + core * SHARD_UNITS
            for n in range(3):
                pair = first // 2 + n
                row = kept[head * 4 + xx, pair // 4]
                unit = head * DENSE_STRIDE + (row + 1) * PER + lax.rem(pair, 4) * 2
                for u in range(2):
                    rows = pl.ds(n * 32 + u * UNIT, UNIT)
                    part[AT[ob], AT[oa], rows] = dense[unit + u]

    def r_copy(oa, i, d, step):
        dest = 4 if step == 0 else d * (4 - step)
        ref, land = part.at[AT[dest], AT[oa]], got.at[AT[oa], i, step]
        if step == 0:
            ref, land = ref.at[pl.ds(i * HALF, HALF)], land.at[pl.ds(i * HALF, HALF)]
        return remote(ref, land, r_send.at[AT[oa], i, step], r_recv.at[AT[oa], i, step], to_b[d])

    def s_copy(i, d, step):
        ref, land = send2.at[i, step], got2.at[i, step]
        if step == 0:
            ref, land = ref.at[pl.ds(i * HALF, HALF)], land.at[pl.ds(i * HALF, HALF)]
        return remote(ref, land, s_send.at[i, step], s_recv.at[i, step], to_a[d])

    REDUCE = (4, 3, -3, 2, -2, 1, -1, 0)

    def r_step(step):
        for oa in REDUCE:
            for i, d in DIRECTIONS:
                if step:
                    r_copy(oa, i, d, step - 1).wait_recv()
                    rows = pl.ds(i * HALF, HALF) if step == 1 else pl.ds(0, SHARD)
                    m = AT[d * (4 - step)]
                    part[m, AT[oa], rows] = (
                        part[m, AT[oa], rows].astype(f32) + got[AT[oa], i, step - 1, rows].astype(f32)
                    ).astype(bf16)
                r_copy(oa, i, d, step).start()

    def r_last(oa):
        for i, d in DIRECTIONS:
            r_copy(oa, i, d, 3).wait_recv()
        j = AT[oa]
        total[j] = part[0, j].astype(f32) + got[j, 0, 3].astype(f32) + got[j, 1, 3].astype(f32)

    def s_step(step):
        for i, d in DIRECTIONS:
            if step == 0:
                rows = pl.ds(i * HALF, HALF)
                send2[i, 0, rows] = total[AT[4], rows].astype(bf16)
            else:
                s_copy(i, d, step - 1).wait_recv()
                j = AT[d * (4 - step)]
                if step == 1:
                    rows, rest = pl.ds(i * HALF, HALF), pl.ds((1 - i) * HALF, HALF)
                    send2[i, 1, rows] = (total[j, rows] + got2[i, 0, rows].astype(f32)).astype(bf16)
                    send2[i, 1, rest] = total[j, rest].astype(bf16)
                else:
                    send2[i, step] = (total[j] + got2[i, step - 1].astype(f32)).astype(bf16)
            s_copy(i, d, step).start()

    k_own = pl.ds(pl.multiple_of(core * 64, 64), 64)

    def block_at(head, row):
        unit = head * HEAD_STRIDE + slot_of[head * 4 + xx, row] * PER
        return jnp.concatenate([w_all[unit + u] for u in range(PER)], axis=0)

    def input_group(group):
        def body(step, carry):
            row = group * 16 + step * 2
            blocks = [
                jnp.concatenate([block_at(0, row + n), block_at(1, row + n)], axis=1) for n in range(2)
            ]
            product = lax.dot_general(
                k_cat[k_own, :], jnp.concatenate(blocks, axis=0), (((1,), (1,)), ((), ())),
                preferred_element_type=f32,
            )
            og[:, pl.ds(pl.multiple_of(row * BLOCK, 256), 256)] = product.astype(bf16)
            return carry

        lax.fori_loop(0, 8, body, 0)

    def own_rows(offset):
        return pl.ds(pl.multiple_of(wrap(xx + offset, XN) * OWN, OWN), OWN)

    def o_copy(i, d, n):
        group = (2 * i + n % 2) if n < 2 or n >= 4 else (2 * (1 - i) + n % 2)
        if n < 2:
            src = og.at[own_rows(2), x_columns(group)]
            dst = xa.at[i, :, x_columns(n)]
        else:
            src = og.at[own_rows(d), x_columns(group)]
            dst = xr.at[i, :, x_columns(group)]
        return remote(src, dst, o_send.at[i, n], o_recv.at[i, n], to_x[d])

    def send_group(group):
        far, n = group // 2, group % 2
        i, d = DIRECTIONS[far]
        o_copy(i, d, n).start()
        i, d = DIRECTIONS[1 - far]
        o_copy(i, d, 2 + n).start()

    def forward_group(n):
        for i, d in DIRECTIONS:
            o_copy(i, d, n).wait_recv()
            columns = x_columns(2 * i + n)
            og[own_rows(d), columns] = (
                og[own_rows(d), columns].astype(f32) + xa[i, :, x_columns(n)].astype(f32)
            ).astype(bf16)
            o_copy(i, d, 4 + n).start()

    pick(4)
    r_step(0)
    for offset in (3, -3, 2, -2, 1, -1, 0):
        pick(offset)
    w_shared = w_all.at[pl.ds(0, HEAD_UNITS)]
    remote(w_shared, w_shared, pw_send, pw_recv, partner).wait()
    r_step(1)

    input_group(0)
    send_group(0)
    input_group(2)
    send_group(2)
    r_step(2)
    input_group(1)
    send_group(1)
    input_group(3)
    send_group(3)
    forward_group(0)
    r_step(3)
    forward_group(1)
    r_last(4)
    s_step(0)
    r_last(3)
    r_last(-3)
    r_last(2)
    r_last(-2)
    s_step(1)
    r_last(1)
    r_last(-1)
    s_step(2)
    r_last(0)
    s_step(3)
    for n in (2, 3, 4, 5):
        for i, d in DIRECTIONS:
            o_copy(i, d, n).wait_recv()
    mine = own_rows(0)

    def finish(step, carry):
        columns = pl.ds(pl.multiple_of(step * 512, 512), 512)
        x_out[:, columns] = (
            og[mine, columns].astype(f32) + xr[0, :, columns].astype(f32) + xr[1, :, columns].astype(f32)
        ).astype(bf16)
        return carry

    lax.fori_loop(0, MODEL_WIDTH // 512, finish, 0)
    for i, d in DIRECTIONS:
        s_copy(i, d, 3).wait_recv()
    scale = 1.0 / math.sqrt(MICRO * 4096)
    w_out[...] = (total[0] + got2[0, 3].astype(f32) + got2[1, 3].astype(f32)) * scale

    for i, d in DIRECTIONS:
        for step in range(4):
            a_copy(i, d, step + 1).wait_send()
            k_copy(i, d, step + 1).wait_send()
            s_copy(i, d, step).wait_send()
            for oa in OFFSETS:
                b_copy(oa, i, d, step + 1).wait_send()
                r_copy(oa, i, d, step).wait_send()
        for n in range(6):
            x_copy(i, d, n).wait_send()
            o_copy(i, d, n).wait_send()


def local(layer_input, key_gradient_rows, key_block_matrix, kept_rows):
    numbers = jnp.arange(1, SLOTS + 1, dtype=jnp.int32)[None, :, None]
    blocks = jnp.arange(BLOCKS, dtype=jnp.int32)[None, None, :]
    slot_of = jnp.sum(jnp.where(kept_rows[:, :, None] == blocks, numbers, 0), axis=1)
    any_space = pl.BlockSpec(memory_space=pl.ANY)
    vmem = pl.BlockSpec(memory_space=pltpu.VMEM)
    dma = pltpu.SemaphoreType.DMA
    weight_grad, input_grad = pl.pallas_call(
        kernel,
        out_shape=(
            jax.ShapeDtypeStruct((SHARD, HEAD_WIDTH), f32),
            jax.ShapeDtypeStruct((OWN, MODEL_WIDTH), bf16),
        ),
        in_specs=[pl.BlockSpec(memory_space=pltpu.SMEM), pl.BlockSpec(memory_space=pltpu.SMEM), any_space, any_space, any_space],
        out_specs=(vmem, vmem),
        scratch_shapes=[
            pltpu.VMEM((2 * HEAD_STRIDE, UNIT, HEAD_WIDTH), bf16),
            pltpu.VMEM((128, MODEL_WIDTH), bf16),
            pltpu.VMEM((2, 2, MICRO, 32, HEAD_WIDTH), bf16),
            pltpu.VMEM((2, 3, 32, HEAD_WIDTH), bf16),
            pltpu.VMEM((128, 2 * HEAD_WIDTH), bf16),
            pltpu.VMEM((2 * DENSE_STRIDE, UNIT, HEAD_WIDTH), bf16),
            pltpu.VMEM((N, N, SHARD, HEAD_WIDTH), bf16),
            pltpu.VMEM((N, 2, 4, SHARD, HEAD_WIDTH), bf16),
            pltpu.VMEM((N, SHARD, HEAD_WIDTH), f32),
            pltpu.VMEM((2, 4, SHARD, HEAD_WIDTH), bf16),
            pltpu.VMEM((2, 4, SHARD, HEAD_WIDTH), bf16),
            pltpu.VMEM((64, MODEL_WIDTH), bf16),
            pltpu.VMEM((2, OWN, MODEL_WIDTH), bf16),
            pltpu.VMEM((2, OWN, MODEL_WIDTH // 2), bf16),
            dma((3,)),
            dma((2, 4)), dma((2, 4)), dma((N, 2, 4)), dma((N, 2, 4)),
            dma, dma, dma, dma, dma((2,)), dma((2,)),
            dma((2, 6)), dma((2, 6)), dma((2, 4)), dma((2, 4)),
            dma((N, 2, 4)), dma((N, 2, 4)), dma((2, 4)), dma((2, 4)), dma((2, 6)), dma((2, 6)),
        ],
        compiler_params=pltpu.CompilerParams(collective_id=0, has_side_effects=True),
    )(
        kept_rows,
        slot_of,
        layer_input.reshape(OWN, MODEL_WIDTH),
        key_gradient_rows,
        key_block_matrix.reshape(SHARD_UNITS, UNIT, HEAD_WIDTH),
    )
    return (
        weight_grad.reshape(1, SHARD, HEAD_WIDTH),
        input_grad.reshape(MICRO, OWN // MICRO, MODEL_WIDTH),
    )


def solution(mesh):
    placed = (
        P(None, ("dp", "tensor"), None),
        P(None, "dp", "tensor"),
        P("tensor", "dp", None),
        P(),
    )
    return jax.shard_map(
        local,
        mesh=mesh,
        in_specs=placed,
        out_specs=(P("tensor", "dp", None), P(None, ("dp", "tensor"), None)),
        check_vma=False,
    )
```

```python
import math

import jax
import jax.numpy as jnp
from jax import lax
from jax.experimental import pallas as pl
from jax.experimental.pallas import tpu as pltpu
from jax.sharding import PartitionSpec as P

MODEL_WIDTH = 8192
HEAD_WIDTH = 128
BLOCK = 128
SLOTS = 48
BLOCKS = MODEL_WIDTH // BLOCK
MICRO = 2
N = 8
XN = 4
SHARD = SLOTS * BLOCK // 64
HALF = SHARD // 2
UNIT = 16
PER = BLOCK // UNIT
SHARD_UNITS = SHARD // UNIT
HEAD_UNITS = SLOTS * PER
HEAD_STRIDE = HEAD_UNITS + PER
DENSE_STRIDE = BLOCKS * PER + PER
OWN = 16
GROUP = MODEL_WIDTH // 4
MESH = pl.DeviceIdType.MESH
OFFSETS = (0, 1, -1, 2, -2, 3, -3, 4)
AT = {offset: index for index, offset in enumerate(OFFSETS)}
DIRECTIONS = ((0, 1), (1, -1))
X_ORDER = ((0, 1, 2, 3, 0, 1), (2, 3, 0, 1, 2, 3))
f32, bf16 = jnp.float32, jnp.bfloat16


def wrap(value, size):
    return lax.rem(value + size, size)


def kernel(
    kept, slot_of, x_in, k_in, w_in, w_out, x_out,
    w_all, x_all, k_raw, k_cat, dense, part, got, total, got2, send2, og, xr, xa,
    local_sem, a_send, a_recv, b_send, b_recv, pw_send, pw_recv, px_send, px_recv, pk_send, pk_recv,
    x_send, x_recv, kc_send, kc_recv, r_send, r_recv, s_send, s_recv, o_send, o_recv,
):
    dp, tp = lax.axis_index("dp"), lax.axis_index("tensor")
    y, zl, core = dp // 8, lax.rem(dp // 2, 4), lax.rem(dp, 2)
    zh, xx = tp // 4, lax.rem(tp, 4)
    z = zh * 4 + zl
    a = y + core * (z - y)
    b = z + core * (y - z)

    def device(y_, z_, core_, x_):
        return (y_ * 8 + lax.rem(z_, 4) * 2 + core_, (z_ // 4) * 4 + x_)

    def device_ab(a_, b_):
        return device(a_ + core * (b_ - a_), b_ + core * (a_ - b_), core, xx)

    a_at = {o: wrap(a + o, N) for o in OFFSETS}
    b_at = {o: wrap(b + o, N) for o in OFFSETS}

    def y_rows(y_):
        return y_ * (768 // UNIT)

    def z_rows(z_):
        return (z_ // 4) * HEAD_STRIDE + PER + lax.rem(z_, 4) * (192 // UNIT)

    a_rows = {o: y_rows(v) + core * (z_rows(v) - y_rows(v)) + core * SHARD_UNITS for o, v in a_at.items()}
    b_rows = {o: z_rows(v) + core * (y_rows(v) - z_rows(v)) for o, v in b_at.items()}
    to_a = {o: device_ab(a_at[o], b) for o in OFFSETS if o}
    to_b = {d: device_ab(a, b_at[d]) for d in (1, -1)}
    far_z = device(y, wrap(z + 4, N), core, xx)
    to_x = {d: device(y, z, core, wrap(xx + d, XN)) for d in (1, -1)}
    partner = device(y, z, 1 - core, xx)

    barrier = pltpu.get_barrier_semaphore()
    everyone = (*to_a.values(), *to_b.values(), *to_x.values(), partner, far_z)
    for there in everyone:
        pl.semaphore_signal(barrier, inc=1, device_id=there, device_id_type=MESH)

    def remote(src, dst, send, recv, there):
        return pltpu.make_async_remote_copy(
            src_ref=src, dst_ref=dst, send_sem=send, recv_sem=recv, device_id=there, device_id_type=MESH
        )

    def piece(oa, ob, half=None):
        row = a_rows[oa] + b_rows[ob]
        if half is None:
            return w_all.at[pl.ds(row, SHARD_UNITS)]
        return w_all.at[pl.ds(row + half * (SHARD_UNITS // 2), SHARD_UNITS // 2)]

    def a_copy(o):
        return remote(w_in, piece(0, 0), a_send.at[AT[o]], a_recv.at[AT[o]], to_a[o])

    def b_copy(oa, i, d, hop):
        offset = -d * (hop - 1)
        half = i if hop == 4 else None
        src = w_in if hop == 1 and oa == 0 else piece(oa, offset, half)
        j = AT[oa]
        return remote(
            src, piece(oa, offset, half), b_send.at[j, i, hop - 1], b_recv.at[j, i, hop - 1], to_b[d]
        )

    def share(oa, ob, half=None, src=None):
        ref = piece(oa, ob, half)
        remote(ref if src is None else src, ref, pw_send, pw_recv, partner).start()

    def x_rows(core_, x_):
        return pl.ds(pl.multiple_of(core_ * 64 + x_ * OWN, OWN), OWN)

    def x_columns(group):
        return pl.ds(group * GROUP, GROUP)

    def x_copy(i, d, n):
        columns = x_columns(X_ORDER[i][n])
        if n < 4:
            src, origin = x_in.at[:, columns], xx
        else:
            origin = wrap(xx - d, XN)
            src = x_all.at[x_rows(core, origin), columns]
        return remote(
            src, x_all.at[x_rows(core, origin), columns], x_send.at[i, n], x_recv.at[i, n], to_x[d]
        )

    def share_x(i, d, n):
        origin = wrap(xx - d, XN) if n < 4 else wrap(xx - 2 * d, XN)
        ref = x_all.at[x_rows(core, origin), x_columns(X_ORDER[i][n])]
        remote(ref, ref, px_send, px_recv, partner).start()

    def k_copy():
        src = k_in.at[:, pl.ds(pl.multiple_of((1 - zh) * 32, 32), 32)]
        return remote(src, k_raw.at[core, zh], kc_send, kc_recv, far_z)

    def k_share(own):
        if own:
            src = k_in.at[:, pl.ds(pl.multiple_of(zh * 32, 32), 32)]
            return remote(src, k_raw.at[core, zh], pk_send.at[0], pk_recv.at[0], partner)
        ref = k_raw.at[core, 1 - zh]
        return remote(ref, ref, pk_send.at[1], pk_recv.at[1], partner)

    local = [
        pltpu.make_async_copy(w_in, piece(0, 0), local_sem.at[0]),
        pltpu.make_async_copy(x_in, x_all.at[x_rows(core, xx)], local_sem.at[1]),
        pltpu.make_async_copy(
            k_in.at[:, pl.ds(pl.multiple_of(zh * 32, 32), 32)], k_raw.at[core, zh], local_sem.at[2]
        ),
    ]
    for copy in local:
        copy.start()
    for head in range(2):
        w_all[pl.ds(head * HEAD_STRIDE, PER)] = jnp.zeros((PER, UNIT, HEAD_WIDTH), bf16)
        dense[pl.ds(head * DENSE_STRIDE, PER)] = jnp.zeros((PER, UNIT, HEAD_WIDTH), bf16)

    pl.semaphore_wait(barrier, len(everyone))

    for o in (1, -1):
        a_copy(o).start()
    for i, d in DIRECTIONS:
        b_copy(0, i, d, 1).start()
    k_copy().start()
    for o in (2, -2, 3, -3, 4):
        a_copy(o).start()
    for n in range(4):
        for i, d in DIRECTIONS:
            x_copy(i, d, n).start()
    share(0, 0, src=w_in)
    k_share(True).start()
    remote(x_in, x_all.at[x_rows(core, xx)], px_send, px_recv, partner).start()

    def a_arrival(oa):
        a_copy(-oa if oa != 4 else 4).wait_recv()
        for i, d in DIRECTIONS:
            b_copy(oa, i, d, 1).start()
        share(oa, 0)

    def b_arrival(oa, hop):
        for i, d in DIRECTIONS:
            b_copy(oa, i, d, hop).wait_recv()
            if hop < 4:
                b_copy(oa, i, d, hop + 1).start()
                share(oa, -d * hop)
            else:
                share(oa, 4, i)

    def x_arrival(n):
        for i, d in DIRECTIONS:
            x_copy(i, d, n).wait_recv()
            if n < 2:
                x_copy(i, d, n + 4).start()
            share_x(i, d, n)

    def k_arrival():
        k_copy().wait_recv()
        k_share(False).start()

    events = [(5.2, k_arrival, ())]
    for n in range(6):
        events.append((4.2 + 1.45 * n, x_arrival, (n,)))
    for oa in OFFSETS:
        first = 2.4 + 0.9 * abs(oa) if oa else 0.0
        if oa:
            events.append((first, a_arrival, (oa,)))
        for hop in range(1, 5):
            events.append((first + 3.0 * hop, b_arrival, (oa, hop)))
    for _, event, arguments in sorted(events, key=lambda entry: entry[0]):
        event(*arguments)

    for copy in local:
        copy.wait()
    k_share(True).wait()
    k_share(False).wait()
    for core_ in range(2):
        for head in range(2):
            raw = k_raw[core_, head].astype(f32)
            rows = [raw[m, x_ * 8:x_ * 8 + 8] for x_ in range(XN) for m in range(MICRO)]
            k_cat[core_ * 64:core_ * 64 + 64, head * 128:head * 128 + 128] = jnp.concatenate(
                rows, axis=0
            ).astype(bf16)
    x_shared = x_all.at[pl.ds(0, 64)]
    remote(x_shared, x_shared, px_send, px_recv, partner).wait()

    width = 512

    def dense_step(step, carry):
        columns = pl.ds(pl.multiple_of(step * width, width), width)
        product = lax.dot_general(
            x_all[:, columns], k_cat[...], (((0,), (0,)), ((), ())), preferred_element_type=f32
        ).astype(bf16)
        for head in range(2):
            rows = pl.ds(head * DENSE_STRIDE + PER + step * (width // UNIT), width // UNIT)
            dense[rows] = product[:, head * 128:head * 128 + 128].reshape(width // UNIT, UNIT, HEAD_WIDTH)
        return carry

    lax.fori_loop(0, MODEL_WIDTH // width, dense_step, 0)

    def pick(ob):
        for oa in OFFSETS:
            y_ = a_at[oa] + core * (b_at[ob] - a_at[oa])
            z_ = b_at[ob] + core * (a_at[oa] - b_at[ob])
            head = z_ // 4
            first = y_ * 48 + lax.rem(z_, 4) * 12 + core * SHARD_UNITS
            for n in range(3):
                pair = first // 2 + n
                row = kept[head * 4 + xx, pair // 4]
                unit = head * DENSE_STRIDE + (row + 1) * PER + lax.rem(pair, 4) * 2
                for u in range(2):
                    rows = pl.ds(n * 32 + u * UNIT, UNIT)
                    part[AT[ob], AT[oa], rows] = dense[unit + u]

    def r_copy(oa, i, d, step):
        dest = 4 if step == 0 else d * (4 - step)
        ref, land = part.at[AT[dest], AT[oa]], got.at[AT[oa], i, step]
        if step == 0:
            ref, land = ref.at[pl.ds(i * HALF, HALF)], land.at[pl.ds(i * HALF, HALF)]
        return remote(ref, land, r_send.at[AT[oa], i, step], r_recv.at[AT[oa], i, step], to_b[d])

    def s_copy(o):
        return remote(send2.at[AT[o]], got2.at[AT[o]], s_send.at[AT[o]], s_recv.at[AT[o]], to_a[o])

    REDUCE = (4, 3, -3, 2, -2, 1, -1, 0)

    def r_step(step):
        for oa in REDUCE:
            for i, d in DIRECTIONS:
                if step:
                    r_copy(oa, i, d, step - 1).wait_recv()
                    rows = pl.ds(i * HALF, HALF) if step == 1 else pl.ds(0, SHARD)
                    m = AT[d * (4 - step)]
                    part[m, AT[oa], rows] = (
                        part[m, AT[oa], rows].astype(f32) + got[AT[oa], i, step - 1, rows].astype(f32)
                    ).astype(bf16)
                r_copy(oa, i, d, step).start()

    def r_last(oa):
        for i, d in DIRECTIONS:
            r_copy(oa, i, d, 3).wait_recv()
        j = AT[oa]
        sums = part[0, j].astype(f32) + got[j, 0, 3].astype(f32) + got[j, 1, 3].astype(f32)
        if oa:
            send2[j] = sums.astype(bf16)
            s_copy(oa).start()
        else:
            total[...] = sums

    k_own = pl.ds(pl.multiple_of(core * 64, 64), 64)

    def block_at(head, row):
        unit = head * HEAD_STRIDE + slot_of[head * 4 + xx, row] * PER
        return jnp.concatenate([w_all[unit + u] for u in range(PER)], axis=0)

    def input_group(group):
        def body(step, carry):
            row = group * 16 + step * 2
            blocks = [
                jnp.concatenate([block_at(0, row + n), block_at(1, row + n)], axis=1) for n in range(2)
            ]
            product = lax.dot_general(
                k_cat[k_own, :], jnp.concatenate(blocks, axis=0), (((1,), (1,)), ((), ())),
                preferred_element_type=f32,
            )
            og[:, pl.ds(pl.multiple_of(row * BLOCK, 256), 256)] = product.astype(bf16)
            return carry

        lax.fori_loop(0, 8, body, 0)

    def own_rows(offset):
        return pl.ds(pl.multiple_of(wrap(xx + offset, XN) * OWN, OWN), OWN)

    def o_copy(i, d, n):
        group = (2 * i + n % 2) if n < 2 or n >= 4 else (2 * (1 - i) + n % 2)
        if n < 2:
            src = og.at[own_rows(2), x_columns(group)]
            dst = xa.at[i, :, x_columns(n)]
        else:
            src = og.at[own_rows(d), x_columns(group)]
            dst = xr.at[i, :, x_columns(group)]
        return remote(src, dst, o_send.at[i, n], o_recv.at[i, n], to_x[d])

    def send_group(group):
        far, n = group // 2, group % 2
        i, d = DIRECTIONS[far]
        o_copy(i, d, n).start()
        i, d = DIRECTIONS[1 - far]
        o_copy(i, d, 2 + n).start()

    def forward_group(n):
        for i, d in DIRECTIONS:
            o_copy(i, d, n).wait_recv()
            columns = x_columns(2 * i + n)
            og[own_rows(d), columns] = (
                og[own_rows(d), columns].astype(f32) + xa[i, :, x_columns(n)].astype(f32)
            ).astype(bf16)
            o_copy(i, d, 4 + n).start()

    pick(4)
    r_step(0)
    for offset in (3, -3, 2, -2, 1, -1, 0):
        pick(offset)
    w_shared = w_all.at[pl.ds(0, HEAD_UNITS)]
    remote(w_shared, w_shared, pw_send, pw_recv, partner).wait()
    r_step(1)

    input_group(0)
    send_group(0)
    input_group(2)
    send_group(2)
    r_step(2)
    input_group(1)
    send_group(1)
    input_group(3)
    send_group(3)
    forward_group(0)
    r_step(3)
    forward_group(1)
    for offset in REDUCE:
        r_last(offset)
    for n in (2, 3, 4, 5):
        for i, d in DIRECTIONS:
            o_copy(i, d, n).wait_recv()
    mine = own_rows(0)

    def finish(step, carry):
        columns = pl.ds(pl.multiple_of(step * 512, 512), 512)
        x_out[:, columns] = (
            og[mine, columns].astype(f32) + xr[0, :, columns].astype(f32) + xr[1, :, columns].astype(f32)
        ).astype(bf16)
        return carry

    lax.fori_loop(0, MODEL_WIDTH // 512, finish, 0)
    sums = total[...]
    for o in OFFSETS[1:]:
        s_copy(o).wait_recv()
        sums = sums + got2[AT[o]].astype(f32)
    w_out[...] = sums * (1.0 / math.sqrt(MICRO * 4096))

    k_copy().wait_send()
    for o in OFFSETS[1:]:
        a_copy(o).wait_send()
        s_copy(o).wait_send()
    for i, d in DIRECTIONS:
        for step in range(4):
            for oa in OFFSETS:
                b_copy(oa, i, d, step + 1).wait_send()
                r_copy(oa, i, d, step).wait_send()
        for n in range(6):
            x_copy(i, d, n).wait_send()
            o_copy(i, d, n).wait_send()


def local(layer_input, key_gradient_rows, key_block_matrix, kept_rows):
    numbers = jnp.arange(1, SLOTS + 1, dtype=jnp.int32)[None, :, None]
    blocks = jnp.arange(BLOCKS, dtype=jnp.int32)[None, None, :]
    slot_of = jnp.sum(jnp.where(kept_rows[:, :, None] == blocks, numbers, 0), axis=1)
    any_space = pl.BlockSpec(memory_space=pl.ANY)
    vmem = pl.BlockSpec(memory_space=pltpu.VMEM)
    dma = pltpu.SemaphoreType.DMA
    weight_grad, input_grad = pl.pallas_call(
        kernel,
        out_shape=(
            jax.ShapeDtypeStruct((SHARD, HEAD_WIDTH), f32),
            jax.ShapeDtypeStruct((OWN, MODEL_WIDTH), bf16),
        ),
        in_specs=[pl.BlockSpec(memory_space=pltpu.SMEM), pl.BlockSpec(memory_space=pltpu.SMEM), any_space, any_space, any_space],
        out_specs=(vmem, vmem),
        scratch_shapes=[
            pltpu.VMEM((2 * HEAD_STRIDE, UNIT, HEAD_WIDTH), bf16),
            pltpu.VMEM((128, MODEL_WIDTH), bf16),
            pltpu.VMEM((2, 2, MICRO, 32, HEAD_WIDTH), bf16),
            pltpu.VMEM((128, 2 * HEAD_WIDTH), bf16),
            pltpu.VMEM((2 * DENSE_STRIDE, UNIT, HEAD_WIDTH), bf16),
            pltpu.VMEM((N, N, SHARD, HEAD_WIDTH), bf16),
            pltpu.VMEM((N, 2, 4, SHARD, HEAD_WIDTH), bf16),
            pltpu.VMEM((SHARD, HEAD_WIDTH), f32),
            pltpu.VMEM((N, SHARD, HEAD_WIDTH), bf16),
            pltpu.VMEM((N, SHARD, HEAD_WIDTH), bf16),
            pltpu.VMEM((64, MODEL_WIDTH), bf16),
            pltpu.VMEM((2, OWN, MODEL_WIDTH), bf16),
            pltpu.VMEM((2, OWN, MODEL_WIDTH // 2), bf16),
            dma((3,)),
            dma((N,)), dma((N,)), dma((N, 2, 4)), dma((N, 2, 4)),
            dma, dma, dma, dma, dma((2,)), dma((2,)),
            dma((2, 6)), dma((2, 6)), dma, dma,
            dma((N, 2, 4)), dma((N, 2, 4)), dma((N,)), dma((N,)), dma((2, 6)), dma((2, 6)),
        ],
        compiler_params=pltpu.CompilerParams(collective_id=0, has_side_effects=True),
    )(
        kept_rows,
        slot_of,
        layer_input.reshape(OWN, MODEL_WIDTH),
        key_gradient_rows,
        key_block_matrix.reshape(SHARD_UNITS, UNIT, HEAD_WIDTH),
    )
    return (
        weight_grad.reshape(1, SHARD, HEAD_WIDTH),
        input_grad.reshape(MICRO, OWN // MICRO, MODEL_WIDTH),
    )


def solution(mesh):
    placed = (
        P(None, ("dp", "tensor"), None),
        P(None, "dp", "tensor"),
        P("tensor", "dp", None),
        P(),
    )
    return jax.shard_map(
        local,
        mesh=mesh,
        in_specs=placed,
        out_specs=(P("tensor", "dp", None), P(None, ("dp", "tensor"), None)),
        check_vma=False,
    )
```

```python
import math

import jax
import jax.numpy as jnp
from jax import lax
from jax.experimental import pallas as pl
from jax.experimental.pallas import tpu as pltpu
from jax.sharding import PartitionSpec as P

MODEL_WIDTH = 8192
HEAD_WIDTH = 128
BLOCK = 128
SLOTS = 48
BLOCKS = MODEL_WIDTH // BLOCK
MICRO = 2
N = 8
XN = 4
SHARD = SLOTS * BLOCK // 64
HALF = SHARD // 2
UNIT = 16
PER = BLOCK // UNIT
SHARD_UNITS = SHARD // UNIT
HEAD_UNITS = SLOTS * PER
HEAD_STRIDE = HEAD_UNITS + PER
DENSE_STRIDE = BLOCKS * PER + PER
OWN = 16
GROUP = MODEL_WIDTH // 4
MESH = pl.DeviceIdType.MESH
OFFSETS = (0, 1, -1, 2, -2, 3, -3, 4)
AT = {offset: index for index, offset in enumerate(OFFSETS)}
DIRECTIONS = ((0, 1), (1, -1))
HOP, T_D, T_R, T_I = 3.3, 13.2, 15.9, 20.5
X_ORDER = ((0, 1, 2, 3, 0, 1), (2, 3, 0, 1, 2, 3))
f32, bf16 = jnp.float32, jnp.bfloat16


def wrap(value, size):
    return lax.rem(value + size, size)


def kernel(
    kept, slot_of, x_in, k_in, w_in, w_out, x_out,
    w_all, x_all, k_raw, k_cat, dense, part, got, total, got2, send2, og, xr, xa,
    local_sem, a_send, a_recv, b_send, b_recv, pw_send, pw_recv, px_send, px_recv, pk_send, pk_recv,
    x_send, x_recv, kc_send, kc_recv, r_send, r_recv, s_send, s_recv, o_send, o_recv,
):
    dp, tp = lax.axis_index("dp"), lax.axis_index("tensor")
    y, zl, core = dp // 8, lax.rem(dp // 2, 4), lax.rem(dp, 2)
    zh, xx = tp // 4, lax.rem(tp, 4)
    z = zh * 4 + zl
    a = y + core * (z - y)
    b = z + core * (y - z)

    def device(y_, z_, core_, x_):
        return (y_ * 8 + lax.rem(z_, 4) * 2 + core_, (z_ // 4) * 4 + x_)

    def device_ab(a_, b_):
        return device(a_ + core * (b_ - a_), b_ + core * (a_ - b_), core, xx)

    a_at = {o: wrap(a + o, N) for o in OFFSETS}
    b_at = {o: wrap(b + o, N) for o in OFFSETS}

    def y_rows(y_):
        return y_ * (768 // UNIT)

    def z_rows(z_):
        return (z_ // 4) * HEAD_STRIDE + PER + lax.rem(z_, 4) * (192 // UNIT)

    a_rows = {o: y_rows(v) + core * (z_rows(v) - y_rows(v)) + core * SHARD_UNITS for o, v in a_at.items()}
    b_rows = {o: z_rows(v) + core * (y_rows(v) - z_rows(v)) for o, v in b_at.items()}
    to_a = {o: device_ab(a_at[o], b) for o in OFFSETS if o}
    to_b = {d: device_ab(a, b_at[d]) for d in (1, -1)}
    far_z = device(y, wrap(z + 4, N), core, xx)
    to_x = {d: device(y, z, core, wrap(xx + d, XN)) for d in (1, -1)}
    partner = device(y, z, 1 - core, xx)

    barrier = pltpu.get_barrier_semaphore()
    everyone = (*to_a.values(), *to_b.values(), *to_x.values(), partner, far_z)
    for there in everyone:
        pl.semaphore_signal(barrier, inc=1, device_id=there, device_id_type=MESH)

    def remote(src, dst, send, recv, there):
        return pltpu.make_async_remote_copy(
            src_ref=src, dst_ref=dst, send_sem=send, recv_sem=recv, device_id=there, device_id_type=MESH
        )

    def piece(oa, ob, half=None):
        row = a_rows[oa] + b_rows[ob]
        if half is None:
            return w_all.at[pl.ds(row, SHARD_UNITS)]
        return w_all.at[pl.ds(row + half * (SHARD_UNITS // 2), SHARD_UNITS // 2)]

    def a_copy(o):
        return remote(w_in, piece(0, 0), a_send.at[AT[o]], a_recv.at[AT[o]], to_a[o])

    def b_copy(oa, i, d, hop):
        offset = -d * (hop - 1)
        half = i if hop == 4 else None
        src = w_in if hop == 1 and oa == 0 else piece(oa, offset, half)
        j = AT[oa]
        return remote(
            src, piece(oa, offset, half), b_send.at[j, i, hop - 1], b_recv.at[j, i, hop - 1], to_b[d]
        )

    def share(oa, ob, half=None, src=None):
        ref = piece(oa, ob, half)
        remote(ref if src is None else src, ref, pw_send, pw_recv, partner).start()

    def x_rows(core_, x_):
        return pl.ds(pl.multiple_of(core_ * 64 + x_ * OWN, OWN), OWN)

    def x_columns(group):
        return pl.ds(group * GROUP, GROUP)

    def x_copy(i, d, n):
        columns = x_columns(X_ORDER[i][n])
        if n < 4:
            src, origin = x_in.at[:, columns], xx
        else:
            origin = wrap(xx - d, XN)
            src = x_all.at[x_rows(core, origin), columns]
        return remote(
            src, x_all.at[x_rows(core, origin), columns], x_send.at[i, n], x_recv.at[i, n], to_x[d]
        )

    def share_x(i, d, n):
        origin = wrap(xx - d, XN) if n < 4 else wrap(xx - 2 * d, XN)
        ref = x_all.at[x_rows(core, origin), x_columns(X_ORDER[i][n])]
        remote(ref, ref, px_send, px_recv, partner).start()

    def k_copy():
        src = k_in.at[:, pl.ds(pl.multiple_of((1 - zh) * 32, 32), 32)]
        return remote(src, k_raw.at[core, zh], kc_send, kc_recv, far_z)

    def k_share(own):
        if own:
            src = k_in.at[:, pl.ds(pl.multiple_of(zh * 32, 32), 32)]
            return remote(src, k_raw.at[core, zh], pk_send.at[0], pk_recv.at[0], partner)
        ref = k_raw.at[core, 1 - zh]
        return remote(ref, ref, pk_send.at[1], pk_recv.at[1], partner)

    local = [
        pltpu.make_async_copy(w_in, piece(0, 0), local_sem.at[0]),
        pltpu.make_async_copy(x_in, x_all.at[x_rows(core, xx)], local_sem.at[1]),
        pltpu.make_async_copy(
            k_in.at[:, pl.ds(pl.multiple_of(zh * 32, 32), 32)], k_raw.at[core, zh], local_sem.at[2]
        ),
    ]
    for copy in local:
        copy.start()
    for head in range(2):
        w_all[pl.ds(head * HEAD_STRIDE, PER)] = jnp.zeros((PER, UNIT, HEAD_WIDTH), bf16)
        dense[pl.ds(head * DENSE_STRIDE, PER)] = jnp.zeros((PER, UNIT, HEAD_WIDTH), bf16)

    pl.semaphore_wait(barrier, len(everyone))

    for o in (1, -1):
        a_copy(o).start()
    for i, d in DIRECTIONS:
        b_copy(0, i, d, 1).start()
    k_copy().start()
    for o in (2, -2, 3, -3, 4):
        a_copy(o).start()
    for n in range(4):
        for i, d in DIRECTIONS:
            x_copy(i, d, n).start()
    share(0, 0, src=w_in)
    k_share(True).start()
    remote(x_in, x_all.at[x_rows(core, xx)], px_send, px_recv, partner).start()

    def a_arrival(oa):
        a_copy(-oa if oa != 4 else 4).wait_recv()
        for i, d in DIRECTIONS:
            b_copy(oa, i, d, 1).start()
        share(oa, 0)

    def b_arrival(oa, hop):
        for i, d in DIRECTIONS:
            b_copy(oa, i, d, hop).wait_recv()
            if hop < 4:
                b_copy(oa, i, d, hop + 1).start()
                share(oa, -d * hop)
            else:
                share(oa, 4, i)

    def x_arrival(n):
        for i, d in DIRECTIONS:
            x_copy(i, d, n).wait_recv()
            if n < 2:
                x_copy(i, d, n + 4).start()
            share_x(i, d, n)

    def k_arrival():
        k_copy().wait_recv()
        k_share(False).start()

    def prepare():
        for copy in local:
            copy.wait()
        k_share(True).wait()
        k_share(False).wait()
        for core_ in range(2):
            for head in range(2):
                raw = k_raw[core_, head].astype(f32)
                rows = [raw[m, x_ * 8:x_ * 8 + 8] for x_ in range(XN) for m in range(MICRO)]
                k_cat[core_ * 64:core_ * 64 + 64, head * 128:head * 128 + 128] = jnp.concatenate(
                    rows, axis=0
                ).astype(bf16)
        x_shared = x_all.at[pl.ds(0, 64)]
        remote(x_shared, x_shared, px_send, px_recv, partner).wait()

    width = 512

    def dense_step(step, carry):
        columns = pl.ds(pl.multiple_of(step * width, width), width)
        product = lax.dot_general(
            x_all[:, columns], k_cat[...], (((0,), (0,)), ((), ())), preferred_element_type=f32
        ).astype(bf16)
        for head in range(2):
            rows = pl.ds(head * DENSE_STRIDE + PER + step * (width // UNIT), width // UNIT)
            dense[rows] = product[:, head * 128:head * 128 + 128].reshape(width // UNIT, UNIT, HEAD_WIDTH)
        return carry

    def dense_part(part_):
        steps = MODEL_WIDTH // width // 4
        lax.fori_loop(part_ * steps, (part_ + 1) * steps, dense_step, 0, unroll=True)

    def pick(*which):
        for ob in which:
            pick_one(ob)

    def pick_one(ob):
        for oa in OFFSETS:
            y_ = a_at[oa] + core * (b_at[ob] - a_at[oa])
            z_ = b_at[ob] + core * (a_at[oa] - b_at[ob])
            head = z_ // 4
            first = y_ * 48 + lax.rem(z_, 4) * 12 + core * SHARD_UNITS
            for n in range(3):
                pair = first // 2 + n
                row = kept[head * 4 + xx, pair // 4]
                unit = head * DENSE_STRIDE + (row + 1) * PER + lax.rem(pair, 4) * 2
                for u in range(2):
                    rows = pl.ds(n * 32 + u * UNIT, UNIT)
                    part[AT[ob], AT[oa], rows] = dense[unit + u]

    def r_copy(oa, i, d, step):
        dest = 4 if step == 0 else d * (4 - step)
        ref, land = part.at[AT[dest], AT[oa]], got.at[AT[oa], i, step]
        if step == 0:
            ref, land = ref.at[pl.ds(i * HALF, HALF)], land.at[pl.ds(i * HALF, HALF)]
        return remote(ref, land, r_send.at[AT[oa], i, step], r_recv.at[AT[oa], i, step], to_b[d])

    def s_copy(o):
        return remote(send2.at[AT[o]], got2.at[AT[o]], s_send.at[AT[o]], s_recv.at[AT[o]], to_a[o])

    REDUCE = (4, 3, -3, 2, -2, 1, -1, 0)

    def r_step(step, which):
        for oa in which:
            for i, d in DIRECTIONS:
                if step:
                    r_copy(oa, i, d, step - 1).wait_recv()
                    rows = pl.ds(i * HALF, HALF) if step == 1 else pl.ds(0, SHARD)
                    m = AT[d * (4 - step)]
                    part[m, AT[oa], rows] = (
                        part[m, AT[oa], rows].astype(f32) + got[AT[oa], i, step - 1, rows].astype(f32)
                    ).astype(bf16)
                r_copy(oa, i, d, step).start()

    def r_last(oa):
        for i, d in DIRECTIONS:
            r_copy(oa, i, d, 3).wait_recv()
        j = AT[oa]
        sums = part[0, j].astype(f32) + got[j, 0, 3].astype(f32) + got[j, 1, 3].astype(f32)
        if oa:
            send2[j] = sums.astype(bf16)
            s_copy(oa).start()
        else:
            total[...] = sums

    k_own = pl.ds(pl.multiple_of(core * 64, 64), 64)

    def block_at(head, row):
        unit = head * HEAD_STRIDE + slot_of[head * 4 + xx, row] * PER
        return jnp.concatenate([w_all[unit + u] for u in range(PER)], axis=0)

    def input_group(group):
        def body(step, carry):
            row = group * 16 + step * 2
            blocks = [
                jnp.concatenate([block_at(0, row + n), block_at(1, row + n)], axis=1) for n in range(2)
            ]
            product = lax.dot_general(
                k_cat[k_own, :], jnp.concatenate(blocks, axis=0), (((1,), (1,)), ((), ())),
                preferred_element_type=f32,
            )
            og[:, pl.ds(pl.multiple_of(row * BLOCK, 256), 256)] = product.astype(bf16)
            return carry

        lax.fori_loop(0, 8, body, 0, unroll=True)

    def own_rows(offset):
        return pl.ds(pl.multiple_of(wrap(xx + offset, XN) * OWN, OWN), OWN)

    def o_copy(i, d, n):
        group = (2 * i + n % 2) if n < 2 or n >= 4 else (2 * (1 - i) + n % 2)
        if n < 2:
            src = og.at[own_rows(2), x_columns(group)]
            dst = xa.at[i, :, x_columns(n)]
        else:
            src = og.at[own_rows(d), x_columns(group)]
            dst = xr.at[i, :, x_columns(group)]
        return remote(src, dst, o_send.at[i, n], o_recv.at[i, n], to_x[d])

    def send_group(group):
        far, n = group // 2, group % 2
        i, d = DIRECTIONS[far]
        o_copy(i, d, n).start()
        i, d = DIRECTIONS[1 - far]
        o_copy(i, d, 2 + n).start()

    def forward_group(n):
        for i, d in DIRECTIONS:
            o_copy(i, d, n).wait_recv()
            columns = x_columns(2 * i + n)
            og[own_rows(d), columns] = (
                og[own_rows(d), columns].astype(f32) + xa[i, :, x_columns(n)].astype(f32)
            ).astype(bf16)
            o_copy(i, d, 4 + n).start()

    def blocks_complete():
        w_shared = w_all.at[pl.ds(0, HEAD_UNITS)]
        remote(w_shared, w_shared, pw_send, pw_recv, partner).wait()

    def input_part(group):
        input_group(group)
        send_group(group)

    events = [(5.2, k_arrival, ())]
    for n in range(6):
        events.append((4.2 + 1.45 * n, x_arrival, (n,)))
    for oa in OFFSETS:
        first = 2.4 + 0.9 * abs(oa) if oa else 0.0
        if oa:
            events.append((first, a_arrival, (oa,)))
        for hop in range(1, 5):
            events.append((first + HOP * hop, b_arrival, (oa, hop)))
    near, rest = REDUCE[:4], REDUCE[4:]
    events += [
        (T_D, prepare, ()),
        (T_D + 0.1, dense_part, (0,)),
        (T_D + 0.7, dense_part, (1,)),
        (T_D + 1.3, dense_part, (2,)),
        (T_D + 1.9, dense_part, (3,)),
        (T_R, pick, (4,)),
        (T_R + 0.1, r_step, (0, REDUCE)),
        (T_R + 0.5, pick, (3, -3)),
        (T_R + 1.0, pick, (2, -2)),
        (T_R + 1.5, pick, (1, -1, 0)),
        (T_R + 2.9, r_step, (1, near)),
        (T_R + 3.4, r_step, (1, rest)),
        (T_R + 5.9, r_step, (2, near)),
        (T_R + 6.6, r_step, (2, rest)),
        (T_R + 9.0, r_step, (3, near)),
        (T_R + 9.7, r_step, (3, rest)),
        (T_I, blocks_complete, ()),
        (T_I + 0.1, input_part, (0,)),
        (T_I + 0.9, input_part, (2,)),
        (T_I + 1.7, input_part, (1,)),
        (T_I + 2.5, input_part, (3,)),
        (T_I + 5.2, forward_group, (0,)),
        (T_I + 7.5, forward_group, (1,)),
    ]
    for n, offset in enumerate(REDUCE):
        events.append((T_R + 12.1 + 0.26 * n, r_last, (offset,)))
    for _, event, arguments in sorted(events, key=lambda entry: entry[0]):
        event(*arguments)

    for n in (2, 3, 4, 5):
        for i, d in DIRECTIONS:
            o_copy(i, d, n).wait_recv()
    mine = own_rows(0)

    def finish(step, carry):
        columns = pl.ds(pl.multiple_of(step * 512, 512), 512)
        x_out[:, columns] = (
            og[mine, columns].astype(f32) + xr[0, :, columns].astype(f32) + xr[1, :, columns].astype(f32)
        ).astype(bf16)
        return carry

    lax.fori_loop(0, MODEL_WIDTH // 512, finish, 0)
    sums = total[...]
    for o in OFFSETS[1:]:
        s_copy(o).wait_recv()
        sums = sums + got2[AT[o]].astype(f32)
    w_out[...] = sums * (1.0 / math.sqrt(MICRO * 4096))

    k_copy().wait_send()
    for o in OFFSETS[1:]:
        a_copy(o).wait_send()
        s_copy(o).wait_send()
    for i, d in DIRECTIONS:
        for step in range(4):
            for oa in OFFSETS:
                b_copy(oa, i, d, step + 1).wait_send()
                r_copy(oa, i, d, step).wait_send()
        for n in range(6):
            x_copy(i, d, n).wait_send()
            o_copy(i, d, n).wait_send()


def local(layer_input, key_gradient_rows, key_block_matrix, kept_rows):
    numbers = jnp.arange(1, SLOTS + 1, dtype=jnp.int32)[None, :, None]
    blocks = jnp.arange(BLOCKS, dtype=jnp.int32)[None, None, :]
    slot_of = jnp.sum(jnp.where(kept_rows[:, :, None] == blocks, numbers, 0), axis=1)
    any_space = pl.BlockSpec(memory_space=pl.ANY)
    vmem = pl.BlockSpec(memory_space=pltpu.VMEM)
    dma = pltpu.SemaphoreType.DMA
    weight_grad, input_grad = pl.pallas_call(
        kernel,
        out_shape=(
            jax.ShapeDtypeStruct((SHARD, HEAD_WIDTH), f32),
            jax.ShapeDtypeStruct((OWN, MODEL_WIDTH), bf16),
        ),
        in_specs=[pl.BlockSpec(memory_space=pltpu.SMEM), pl.BlockSpec(memory_space=pltpu.SMEM), any_space, any_space, any_space],
        out_specs=(vmem, vmem),
        scratch_shapes=[
            pltpu.VMEM((2 * HEAD_STRIDE, UNIT, HEAD_WIDTH), bf16),
            pltpu.VMEM((128, MODEL_WIDTH), bf16),
            pltpu.VMEM((2, 2, MICRO, 32, HEAD_WIDTH), bf16),
            pltpu.VMEM((128, 2 * HEAD_WIDTH), bf16),
            pltpu.VMEM((2 * DENSE_STRIDE, UNIT, HEAD_WIDTH), bf16),
            pltpu.VMEM((N, N, SHARD, HEAD_WIDTH), bf16),
            pltpu.VMEM((N, 2, 4, SHARD, HEAD_WIDTH), bf16),
            pltpu.VMEM((SHARD, HEAD_WIDTH), f32),
            pltpu.VMEM((N, SHARD, HEAD_WIDTH), bf16),
            pltpu.VMEM((N, SHARD, HEAD_WIDTH), bf16),
            pltpu.VMEM((64, MODEL_WIDTH), bf16),
            pltpu.VMEM((2, OWN, MODEL_WIDTH), bf16),
            pltpu.VMEM((2, OWN, MODEL_WIDTH // 2), bf16),
            dma((3,)),
            dma((N,)), dma((N,)), dma((N, 2, 4)), dma((N, 2, 4)),
            dma, dma, dma, dma, dma((2,)), dma((2,)),
            dma((2, 6)), dma((2, 6)), dma, dma,
            dma((N, 2, 4)), dma((N, 2, 4)), dma((N,)), dma((N,)), dma((2, 6)), dma((2, 6)),
        ],
        compiler_params=pltpu.CompilerParams(collective_id=0, has_side_effects=True),
    )(
        kept_rows,
        slot_of,
        layer_input.reshape(OWN, MODEL_WIDTH),
        key_gradient_rows,
        key_block_matrix.reshape(SHARD_UNITS, UNIT, HEAD_WIDTH),
    )
    return (
        weight_grad.reshape(1, SHARD, HEAD_WIDTH),
        input_grad.reshape(MICRO, OWN // MICRO, MODEL_WIDTH),
    )


def solution(mesh):
    placed = (
        P(None, ("dp", "tensor"), None),
        P(None, "dp", "tensor"),
        P("tensor", "dp", None),
        P(),
    )
    return jax.shard_map(
        local,
        mesh=mesh,
        in_specs=placed,
        out_specs=(P("tensor", "dp", None), P(None, ("dp", "tensor"), None)),
        check_vma=False,
    )
```
